512 devices in a mesh: site: 16 (over z), patch: 32 (over x, y, core).
Axes of the slice: x: 4, y: 4, z: 16, core: 2. Of those that a mesh axis runs over, the one named last changes fastest.
Arguments:
- slip_rates: bfloat16 [512, 64, 256], P('patch', 'site'), may hold values from -6 to 6
- green_tiles: bfloat16 [16, 1024, 2, 1024], P('site', 'patch'), may hold values from -0.015625 to 0.015625
- patch_slot: int32 [512], replicated, may hold values from 0 to 1023, as said below
Outputs:
- seismograms: float32 [16, 64, 2, 1280], P('site', 'patch')
The draws below stay inside these ranges and needn't reach their ends.
Inputs may be any that keep to these rules, and one draw needn't show every extreme that they name: The values of patch_slot all differ. Patch p belongs to owner patch_slot[p] // 32 and fills its slot patch_slot[p] % 32; each owner has 1 to 32 patches in its first slots, and some owner has exactly 32. The 16 patches p with the same p // 16 include at most 2 of any one owner, and some such group includes exactly 2 of one owner.
All inputs are finite; a program needn't handle non-finite values.
Results may differ from the reference program's by a relative error of at most 0.0003.
Values may be sent and summed in bfloat16 or wider, within the bound.
A program may use at most 64 MiB of HBM per device.

```python
import jax
import jax.numpy as jnp
from jax import lax

V = 64
SAMPLES = 256
LAGS = 1024
PATCH_DEV = 16
PATCHES = 512
SLOTS = 1024
SITES = 16
OUT = 1280


def draw_patch_slot(key, part):
    sources = PATCHES // PATCH_DEV
    per_source = PATCH_DEV
    half_len = per_source // 2
    slot_width = 2 * per_source
    key_offs, key_heavy, key_perm = jax.random.split(jax.random.fold_in(key, 17), 3)
    offsets = jax.random.randint(key_offs, (sources + 1,), 1 - half_len, half_len)
    heavy_run = jax.random.randint(key_heavy, (), 1, sources - 1)
    mark_index = jnp.arange(sources + 1)
    offsets = jnp.where(mark_index == heavy_run, -half_len, offsets)
    offsets = jnp.where(mark_index == heavy_run + 1, half_len, offsets)
    offsets = jnp.where((mark_index == 0) | (mark_index == sources), 0, offsets)
    cut_points = mark_index * per_source + offsets
    labels = jax.random.permutation(key_perm, sources)
    places = jnp.arange(PATCHES)
    run_of = jnp.sum((places[:, None] >= cut_points[None, 1:sources]).astype(jnp.int32), axis=1)
    slot_at = labels[run_of] * slot_width + places - cut_points[run_of]
    patches = jnp.arange(PATCHES)
    source_of = patches // per_source
    local_of = patches % per_source
    place_of = local_of // 2 * (2 * sources) + 2 * source_of + local_of % 2
    return slot_at[place_of].astype(jnp.int32)


def shard_levels(key, extent, cuts, least, largest):
    def one(position, shards_of):
        draws = jax.random.uniform(jax.random.fold_in(jax.random.fold_in(key, 6), position), (shards_of,), jnp.float32, least / len(cuts), largest / len(cuts))
        return jnp.repeat(jnp.exp(draws), extent[position] // shards_of).reshape((-1,) + (1,) * (len(extent) - position - 1))

    gain = one(*cuts[0])
    for cut in cuts[1:]:
        gain = gain * one(*cut)
    return gain


def noise(rng, shape, spread, reach, cuts=(), held_as=jnp.bfloat16):
    result = spread * jax.random.normal(rng, shape, jnp.float32)
    if cuts:
        result = result * shard_levels(rng, shape, cuts, -0.22, 0.18)
    return jnp.clip(result, -reach, reach).astype(held_as)


def setup_inputs(seed: int = 0) -> dict:
    keys = jax.random.split(jax.random.key(seed), 4)
    return {
        "slip_rates": noise(keys[0], (PATCHES, V, SAMPLES), 1.0, 6.0, ((0, 32), (1, 16))),
        "green_tiles": noise(keys[1], (SITES, SLOTS, 2, LAGS), (PATCHES * SAMPLES) ** -0.5, 0.015625, ((0, 16), (1, 32))),
        "patch_slot": draw_patch_slot(jax.random.fold_in(keys[3], 71), 0),
    }


def reference(slip_rates, green_tiles, patch_slot):
    fft_length = SAMPLES + OUT
    slip_freq = jnp.fft.rfft(slip_rates.astype(jnp.float32), n=fft_length, axis=-1)

    def one_site(site_tiles):
        patch_tiles = jnp.take(site_tiles, patch_slot, axis=0).astype(jnp.float32)
        tile_freq = jnp.fft.rfft(patch_tiles, n=fft_length, axis=-1)
        product = jnp.einsum('pvf,pcf->vcf', slip_freq, tile_freq)
        return jnp.fft.irfft(product, n=fft_length, axis=-1)[..., :OUT]

    return lax.map(one_site, green_tiles)
```

```python
import functools

import jax
import jax.numpy as jnp
from jax import lax
from jax.experimental import pallas as pl
from jax.experimental.pallas import tpu as pltpu
from jax.sharding import PartitionSpec as P

MESH = pl.DeviceIdType.MESH
BLOCK = 32
LANES = 128


def right_slot(k, nz):
    return 2 * k - 1


def left_slot(k, nz):
    return 2 * k


def kernel(
    nz, npd, tab_out, tab_in, slip_ref, green_ref, out_ref,
    gath, outg, arrived, band, prod, part, recv,
    zsend, zrecv, gsend, grecv, rsend, rrecv,
):
    z = lax.axis_index("site")
    me = lax.axis_index("patch")
    patches = tab_in.shape[0]
    lags = green_ref.shape[2]
    tiles = lags // LANES
    width = lags + LANES
    out_len = out_ref.shape[2]
    rows = slip_ref.shape[0]

    barrier = pltpu.get_barrier_semaphore()
    for step in (2, nz - 2, 1, nz - 1):
        pl.semaphore_signal(
            barrier, inc=1, device_id=(lax.rem(z + step, nz), me), device_id_type=MESH
        )

    def greet(i, carry):
        pl.semaphore_signal(
            barrier, inc=1, device_id=(z, lax.rem(me + i, npd)), device_id_type=MESH
        )
        return carry

    lax.fori_loop(1, npd, greet, 0)

    for entry in range(2 * npd):
        outg[entry] = green_ref[tab_out[entry]]
    gath[0] = slip_ref[...]

    pl.semaphore_wait(barrier, npd - 1 + 4)

    def zcopy(direction, k):
        slot_of = right_slot if direction == 1 else left_slot
        hop = 1 if k % 2 else 2
        source = slip_ref if k == hop else gath.at[slot_of(k - hop, nz)]
        slot = slot_of(k, nz)
        target = lax.rem(z + (hop if direction == 1 else nz - hop), nz)
        return pltpu.make_async_remote_copy(
            src_ref=source,
            dst_ref=gath.at[slot],
            send_sem=zsend.at[slot],
            recv_sem=zrecv.at[slot],
            device_id=(target, me),
            device_id_type=MESH,
        )

    reach_right = nz // 2
    reach_left = nz - 1 - reach_right

    def relay(done):
        for k in (done + 2, done + 1):
            if k <= reach_right:
                zcopy(1, k).start()
            if k <= reach_left:
                zcopy(-1, k).start()

    def zwait(k):
        if k <= reach_right:
            zcopy(1, k).wait_recv()
        if k <= reach_left:
            zcopy(-1, k).wait_recv()

    relay(0)

    def gcopy(i):
        peer = lax.rem(me + i, npd)
        return pltpu.make_async_remote_copy(
            src_ref=outg.at[pl.ds(2 * peer, 2)],
            dst_ref=arrived.at[pl.ds(2 * me, 2)],
            send_sem=gsend.at[peer],
            recv_sem=grecv.at[me],
            device_id=(z, peer),
            device_id_type=MESH,
        )

    def gstart(i, carry):
        gcopy(i).start()
        return carry

    lax.fori_loop(1, npd, gstart, 0)
    keep = pltpu.make_async_copy(
        outg.at[pl.ds(2 * me, 2)], arrived.at[pl.ds(2 * me, 2)], grecv.at[me]
    )
    keep.start()

    zwait(2)
    relay(2)

    def gwait(i, carry):
        pltpu.make_async_copy(
            outg.at[pl.ds(2 * i, 2)], arrived.at[pl.ds(2 * i, 2)], grecv.at[i]
        ).wait()
        return carry

    lax.fori_loop(0, npd, gwait, 0)
    zwait(4)
    relay(4)

    row_of = lax.broadcasted_iota(jnp.int32, (BLOCK, LANES), 0)
    lane_of = lax.broadcasted_iota(jnp.int32, (BLOCK, LANES), 1)
    inside = lane_of >= row_of

    def build(p, carry):
        tile = arrived[tab_in[p]].astype(jnp.float32)
        at = pl.multiple_of(p * BLOCK, BLOCK)
        for c in range(2):
            before = jnp.zeros((BLOCK, LANES), jnp.float32)
            for m in range(tiles + 1):
                if m < tiles:
                    row = tile[c : c + 1, m * LANES : (m + 1) * LANES]
                    turned = pltpu.roll(
                        jnp.broadcast_to(row, (BLOCK, LANES)), 0, 1, stride=1, stride_axis=0
                    )
                else:
                    turned = jnp.zeros((BLOCK, LANES), jnp.float32)
                block = jnp.where(inside, turned, before)
                before = turned
                start = c * width + m * LANES
                band[pl.ds(at, BLOCK), start : start + LANES] = block.astype(jnp.bfloat16)
        return carry

    lax.fori_loop(0, patches, build, 0)

    sub = lax.broadcasted_iota(jnp.int32, (8, out_len), 0)
    pad = jnp.zeros((8, LANES), jnp.float32)

    def rcopy(slot, h, chip):
        target = 2 * chip + h
        return target, pltpu.make_async_remote_copy(
            src_ref=part.at[2 * slot + h],
            dst_ref=recv.at[me],
            send_sem=rsend.at[2 * slot + h],
            recv_sem=rrecv.at[me],
            device_id=(z, target),
            device_id_type=MESH,
        )

    def chip_of(slot):
        if slot == 0:
            return z
        k = (slot + 1) // 2
        return lax.rem(z + (nz - k if slot % 2 else k), nz)

    def compute(first, last):
        count = last - first
        left = gath[first:last].reshape(count * rows, gath.shape[2])
        step = 256
        for n in range(0, 2 * width, step):
            prod[0 : count * rows, n : n + step] = jnp.dot(
                left, band[:, n : n + step], preferred_element_type=jnp.float32
            )
        for slot in range(first, last):
            base = (slot - first) * rows
            sums, turned = [], []
            for c in range(2):
                u = [
                    prod[base + 8 * i : base + 8 * i + 8, c * width : (c + 1) * width]
                    for i in range(4)
                ]
                even = jnp.concatenate([u[0], pad], 1) + jnp.concatenate([pad, u[2]], 1)
                odd = jnp.concatenate([u[1], pad], 1) + jnp.concatenate([pad, u[3]], 1)
                total = even + pltpu.roll(odd, 2 * BLOCK, 1)
                sums.append(total)
                turned.append(pltpu.roll(total, BLOCK, 1))
            result = jnp.where(sub < 4, sums[0], pltpu.roll(sums[1], 4, 0)) + jnp.where(
                sub < 4, pltpu.roll(turned[0], 4, 0), turned[1]
            )
            for h in range(2):
                part[2 * slot + h, 0:2] = result[2 * h : 2 * h + 2]
                part[2 * slot + h, 2:4] = result[4 + 2 * h : 6 + 2 * h]
            chip = chip_of(slot)
            for h in range(2):
                target, copy = rcopy(slot, h, chip)

                @pl.when(target != me)
                def _():
                    copy.start()

                @pl.when(target == me)
                def _():
                    pltpu.make_async_copy(
                        part.at[2 * slot + h], recv.at[me], rrecv.at[me]
                    ).start()

    zwait(1)
    compute(0, 5)
    zwait(6)
    relay(6)
    zwait(3)
    compute(5, 9)
    zwait(5)
    compute(9, 13)
    zwait(7)
    zwait(8)
    compute(13, 16)

    def rwait(i, carry):
        pltpu.make_async_copy(part.at[i], recv.at[i], rrecv.at[i]).wait()
        return carry

    lax.fori_loop(0, npd, rwait, 0)
    total = jnp.sum(recv[...], axis=0)
    for v in range(2):
        for c in range(2):
            out_ref[v, c : c + 1] = total[2 * c + v : 2 * c + v + 1]

    for k in range(1, reach_right + 1):
        zcopy(1, k).wait_send()
    for k in range(1, reach_left + 1):
        zcopy(-1, k).wait_send()

    def gdrain(i, carry):
        gcopy(i).wait_send()
        return carry

    lax.fori_loop(1, npd, gdrain, 0)
    for slot in range(nz):
        chip = chip_of(slot)
        for h in range(2):
            target, copy = rcopy(slot, h, chip)

            @pl.when(target != me)
            def _():
                copy.wait_send()


def route_tables(patch_slot, slot_width, devices, me):
    owners = (patch_slot // slot_width).reshape(devices, -1)
    within = (patch_slot % slot_width).reshape(devices, -1)
    count = owners.shape[1]
    earlier = lax.broadcasted_iota(jnp.int32, (count, count), 1) < lax.broadcasted_iota(
        jnp.int32, (count, count), 0
    )
    same = owners[:, :, None] == owners[:, None, :]
    rank = jnp.sum((same & earlier[None]).astype(jnp.int32), axis=2)
    ranks = lax.broadcasted_iota(jnp.int32, (1, 2, 1), 1)
    mine = (owners[:, None, :] == me) & (rank[:, None, :] == ranks)
    tab_out = jnp.sum(jnp.where(mine, within[:, None, :], 0), axis=2).reshape(-1)
    source = lax.broadcasted_iota(jnp.int32, owners.shape, 0)
    tab_in = jnp.sum(jnp.where(source == me, owners * 2 + rank, 0), axis=0)
    return tab_out, tab_in


def local(nz, npd, slip_rates, green_tiles, patch_slot):
    me = lax.axis_index("patch")
    patches, own_v, samples = slip_rates.shape
    slot_width, lags = green_tiles.shape[1], green_tiles.shape[3]
    blocks = samples // BLOCK
    assert own_v == 4 and blocks == 8 and npd == 2 * nz and nz == 16
    tab_out, tab_in = route_tables(patch_slot, slot_width, npd, me)
    rows, depth = blocks * own_v, patches * BLOCK
    chunk = (
        slip_rates.reshape(patches, own_v, blocks, BLOCK).transpose(2, 1, 0, 3).reshape(rows, depth)
    )
    width, out_len = lags + LANES, lags + samples
    vmem = pl.BlockSpec(memory_space=pltpu.VMEM)
    smem = pl.BlockSpec(memory_space=pltpu.SMEM)
    dma = pltpu.SemaphoreType.DMA
    result = pl.pallas_call(
        functools.partial(kernel, nz, npd),
        out_shape=jax.ShapeDtypeStruct((2, 2, out_len), jnp.float32),
        in_specs=[smem, smem, vmem, vmem],
        out_specs=vmem,
        scratch_shapes=[
            pltpu.VMEM((nz, rows, depth), jnp.bfloat16),
            pltpu.VMEM((2 * npd, 2, lags), jnp.bfloat16),
            pltpu.VMEM((2 * npd, 2, lags), jnp.bfloat16),
            pltpu.VMEM((depth, 2 * width), jnp.bfloat16),
            pltpu.VMEM((5 * rows, 2 * width), jnp.float32),
            pltpu.VMEM((2 * nz, 4, out_len), jnp.float32),
            pltpu.VMEM((npd, 4, out_len), jnp.float32),
            dma((nz,)), dma((nz,)), dma((npd,)), dma((npd,)), dma((2 * nz,)), dma((npd,)),
        ],
        compiler_params=pltpu.CompilerParams(collective_id=0, has_side_effects=True),
    )(tab_out, tab_in, chunk, green_tiles[0])
    return result[None]


def solution(mesh):
    in_specs = (P("patch", "site", None), P("site", "patch", None, None), P())
    out_specs = P("site", "patch", None, None)
    return jax.shard_map(
        functools.partial(local, mesh.shape["site"], mesh.shape["patch"]),
        mesh=mesh, in_specs=in_specs, out_specs=out_specs, check_vma=False,
    )
```

```python
import functools

import jax
import jax.numpy as jnp
from jax import lax
from jax.experimental import pallas as pl
from jax.experimental.pallas import tpu as pltpu
from jax.sharding import PartitionSpec as P

MESH = pl.DeviceIdType.MESH
BLOCK = 32
LANES = 128


ARRIVAL = (1, 3, 2, 4, 6, 5, 7, 8)
EAGER = 16


def z_slot(direction, k):
    return 1 + 2 * ARRIVAL.index(k) + (direction < 0)


def z_hop(k):
    return 2 if k == 8 else (3, 1, 1)[k % 3]


def kernel(
    nz, npd, slots_hbm, slip_ref, green_hbm, out_ref,
    slots, green_ref, gath, outg, arrived, band, prod, part, pair, recv,
    lsem, zsend, zrecv, gsend, grecv, psend, precv, rsend, rrecv,
):
    z = lax.axis_index("site")
    me = lax.axis_index("patch")
    side = 4
    chip_x, chip_y, core = me // (2 * side), lax.rem(me // 2, side), lax.rem(me, 2)
    my_chip = me // 2
    partner = me + 1 - 2 * core
    patches = slots.shape[0] // npd
    slot_width = green_ref.shape[0]
    lags = green_ref.shape[2]
    tiles = lags // LANES
    width = lags + LANES
    out_len = out_ref.shape[2]
    rows = slip_ref.shape[0]

    load_slots = pltpu.make_async_copy(slots_hbm, slots, lsem.at[0])
    load_green = pltpu.make_async_copy(green_hbm, green_ref, lsem.at[1])
    load_slots.start()
    load_green.start()

    def distance(offset):
        dx, dy, _ = offset
        return min(dx, side - dx) + min(dy, side - dy)

    offsets = [
        (dx, dy, other)
        for dx in range(side) for dy in range(side) for other in range(2)
    ]
    offsets = sorted(offsets, key=distance, reverse=True)[:-2] + [(0, 0, 1)]

    def peer_at(offset):
        dx, dy, other = offset
        chip = lax.rem(chip_x + dx, side) * side + lax.rem(chip_y + dy, side)
        return 2 * chip + (1 - core if other else core)

    barrier = pltpu.get_barrier_semaphore()
    z_steps = (3, nz - 3, 2, nz - 2, 1, nz - 1)
    for step in z_steps:
        pl.semaphore_signal(
            barrier, inc=1, device_id=(lax.rem(z + step, nz), me), device_id_type=MESH
        )
    for offset in offsets:
        pl.semaphore_signal(
            barrier, inc=1, device_id=(z, peer_at(offset)), device_id_type=MESH
        )

    load_slots.wait()
    load_green.wait()

    def pick(device, carry):
        first, last = jnp.int32(0), jnp.int32(0)
        values = [slots[device * patches + i] for i in range(patches)]
        hits = [value // slot_width == me for value in values]
        for i in range(patches):
            last = jnp.where(hits[i], values[i], last)
            j = patches - 1 - i
            first = jnp.where(hits[j], values[j], first)
        outg[2 * device] = green_ref[first % slot_width]
        outg[2 * device + 1] = green_ref[last % slot_width]
        return carry

    lax.fori_loop(0, npd, pick, 0)
    gath[0] = slip_ref[...]

    pl.semaphore_wait(barrier, npd - 1 + len(z_steps))

    def zcopy(direction, k):
        hop = z_hop(k)
        source = slip_ref if k == hop else gath.at[z_slot(direction, k - hop)]
        slot = z_slot(direction, k)
        target = lax.rem(z + (hop if direction == 1 else nz - hop), nz)
        return pltpu.make_async_remote_copy(
            src_ref=source,
            dst_ref=gath.at[slot],
            send_sem=zsend.at[slot],
            recv_sem=zrecv.at[slot],
            device_id=(target, me),
            device_id_type=MESH,
        )

    reach = {1: nz // 2, -1: nz - 1 - nz // 2}

    def zgo(k):
        for direction in (1, -1):
            if k <= reach[direction]:
                zcopy(direction, k).start()

    def zwait(k):
        for direction in (1, -1):
            if k <= reach[direction]:
                zcopy(direction, k).wait_recv()

    zgo(3)
    zgo(1)

    def gcopy(peer):
        return pltpu.make_async_remote_copy(
            src_ref=outg.at[pl.ds(2 * peer, 2)],
            dst_ref=arrived.at[pl.ds(2 * me, 2)],
            send_sem=gsend.at[peer],
            recv_sem=grecv.at[me],
            device_id=(z, peer),
            device_id_type=MESH,
        )

    for offset in offsets:
        gcopy(peer_at(offset)).start()
    keep = pltpu.make_async_copy(
        outg.at[pl.ds(2 * me, 2)], arrived.at[pl.ds(2 * me, 2)], grecv.at[me]
    )
    keep.start()

    def gwait(i, carry):
        pltpu.make_async_copy(
            outg.at[pl.ds(2 * i, 2)], arrived.at[pl.ds(2 * i, 2)], grecv.at[i]
        ).wait()
        return carry

    row_of = lax.broadcasted_iota(jnp.int32, (BLOCK, LANES), 0)
    lane_of = lax.broadcasted_iota(jnp.int32, (BLOCK, LANES), 1)
    inside = lane_of >= row_of

    def build(p, carry):
        owner = slots[me * patches + p] // slot_width
        rank = jnp.int32(0)
        for i in range(patches):
            same = slots[me * patches + i] // slot_width == owner
            rank = jnp.where(same & (p > i), 1, rank)
        tile = arrived[2 * owner + rank].astype(jnp.float32)
        at = pl.multiple_of(p * BLOCK, BLOCK)
        for c in range(2):
            before = jnp.zeros((BLOCK, LANES), jnp.float32)
            for m in range(tiles + 1):
                if m < tiles:
                    row = tile[c : c + 1, m * LANES : (m + 1) * LANES]
                    turned = pltpu.roll(
                        jnp.broadcast_to(row, (BLOCK, LANES)), 0, 1, stride=1, stride_axis=0
                    )
                else:
                    turned = jnp.zeros((BLOCK, LANES), jnp.float32)
                block = jnp.where(inside, turned, before)
                before = turned
                start = c * width + m * LANES
                band[pl.ds(at, BLOCK), start : start + LANES] = block.astype(jnp.bfloat16)
        return carry

    def prepare():
        lax.fori_loop(0, npd, gwait, 0)
        lax.fori_loop(0, patches, build, 0)

    eager = z < EAGER
    zwait(1)
    zgo(2)
    zwait(3)
    zgo(6)
    zgo(4)
    pl.when(eager)(prepare)
    zwait(4)
    zgo(5)
    zwait(6)
    zgo(8)
    zgo(7)
    pl.when(jnp.logical_not(eager))(prepare)

    sub = lax.broadcasted_iota(jnp.int32, (8, out_len), 0)
    pad = jnp.zeros((8, LANES), jnp.float32)

    def pcopy(slot):
        return pltpu.make_async_remote_copy(
            src_ref=part.at[2 * slot + 1 - core],
            dst_ref=pair.at[slot],
            send_sem=psend.at[slot],
            recv_sem=precv.at[slot],
            device_id=(z, partner),
            device_id_type=MESH,
        )

    def rcopy(slot):
        chip = chip_of(slot)
        return chip, pltpu.make_async_remote_copy(
            src_ref=part.at[2 * slot + core],
            dst_ref=recv.at[my_chip],
            send_sem=rsend.at[slot],
            recv_sem=rrecv.at[my_chip],
            device_id=(z, 2 * chip + core),
            device_id_type=MESH,
        )

    def chip_of(slot):
        if slot == 0:
            return z
        k = ARRIVAL[(slot - 1) // 2]
        return lax.rem(z + (nz - k if slot % 2 else k), nz)

    def compute(first, last):
        count = last - first
        left = gath[first:last].reshape(count * rows, gath.shape[2])
        step = 256
        for n in range(0, 2 * width, step):
            prod[0 : count * rows, n : n + step] = jnp.dot(
                left, band[:, n : n + step], preferred_element_type=jnp.float32
            )
        for slot in range(first, last):
            base = (slot - first) * rows
            sums, turned = [], []
            for c in range(2):
                u = [
                    prod[base + 8 * i : base + 8 * i + 8, c * width : (c + 1) * width]
                    for i in range(4)
                ]
                even = jnp.concatenate([u[0], pad], 1) + jnp.concatenate([pad, u[2]], 1)
                odd = jnp.concatenate([u[1], pad], 1) + jnp.concatenate([pad, u[3]], 1)
                total = even + pltpu.roll(odd, 2 * BLOCK, 1)
                sums.append(total)
                turned.append(pltpu.roll(total, BLOCK, 1))
            result = jnp.where(sub < 4, sums[0], pltpu.roll(sums[1], 4, 0)) + jnp.where(
                sub < 4, pltpu.roll(turned[0], 4, 0), turned[1]
            )
            for h in range(2):
                part[2 * slot + h, 0:2] = result[2 * h : 2 * h + 2]
                part[2 * slot + h, 2:4] = result[4 + 2 * h : 6 + 2 * h]
            pcopy(slot).start()

    def forward(first, last):
        for slot in range(first, last):
            pcopy(slot).wait_recv()
            part[2 * slot + core] = part[2 * slot + core] + pair[slot]
            chip, copy = rcopy(slot)

            @pl.when(chip != my_chip)
            def _():
                copy.start()

            @pl.when(chip == my_chip)
            def _():
                pltpu.make_async_copy(
                    part.at[2 * slot + core], recv.at[my_chip], rrecv.at[my_chip]
                ).start()

    zwait(2)
    compute(0, 7)
    zwait(5)
    compute(7, 13)
    forward(0, 7)
    pl.when(eager)(lambda: forward(7, 13))
    zwait(7)
    zwait(8)
    compute(13, 16)
    pl.when(jnp.logical_not(eager))(lambda: forward(7, 13))
    forward(13, 16)

    def rwait(i, carry):
        pltpu.make_async_copy(part.at[i], recv.at[i], rrecv.at[i]).wait()
        return carry

    lax.fori_loop(0, nz, rwait, 0)
    total = jnp.sum(recv[...], axis=0)
    for v in range(2):
        for c in range(2):
            out_ref[v, c : c + 1] = total[2 * c + v : 2 * c + v + 1]

    for direction in (1, -1):
        for k in range(1, reach[direction] + 1):
            zcopy(direction, k).wait_send()

    def gdrain(i, carry):
        @pl.when(i != me)
        def _():
            gcopy(i).wait_send()

        return carry

    lax.fori_loop(0, npd, gdrain, 0)
    for slot in range(nz):
        pcopy(slot).wait_send()
        chip, copy = rcopy(slot)

        @pl.when(chip != my_chip)
        def _():
            copy.wait_send()


def local(nz, npd, slip_rates, green_tiles, patch_slot):
    patches, own_v, samples = slip_rates.shape
    lags = green_tiles.shape[3]
    blocks = samples // BLOCK
    assert own_v == 4 and blocks == 8 and npd == 2 * nz and nz == 16
    rows, depth = blocks * own_v, patches * BLOCK
    chunk = (
        slip_rates.reshape(patches, own_v, blocks, BLOCK).transpose(2, 1, 0, 3).reshape(rows, depth)
    )
    width, out_len = lags + LANES, lags + samples
    vmem = pl.BlockSpec(memory_space=pltpu.VMEM)
    hbm = pl.BlockSpec(memory_space=pltpu.HBM)
    dma = pltpu.SemaphoreType.DMA
    result = pl.pallas_call(
        functools.partial(kernel, nz, npd),
        out_shape=jax.ShapeDtypeStruct((2, 2, out_len), jnp.float32),
        in_specs=[hbm, vmem, hbm],
        out_specs=vmem,
        scratch_shapes=[
            pltpu.SMEM(patch_slot.shape, jnp.int32),
            pltpu.VMEM(green_tiles.shape[1:], jnp.bfloat16),
            pltpu.VMEM((nz, rows, depth), jnp.bfloat16),
            pltpu.VMEM((2 * npd, 2, lags), jnp.bfloat16),
            pltpu.VMEM((2 * npd, 2, lags), jnp.bfloat16),
            pltpu.VMEM((depth, 2 * width), jnp.bfloat16),
            pltpu.VMEM((7 * rows, 2 * width), jnp.float32),
            pltpu.VMEM((2 * nz, 4, out_len), jnp.float32),
            pltpu.VMEM((nz, 4, out_len), jnp.float32),
            pltpu.VMEM((nz, 4, out_len), jnp.float32),
            dma((2,)), dma((nz,)), dma((nz,)), dma((npd,)), dma((npd,)),
            dma((nz,)), dma((nz,)), dma((nz,)), dma((nz,)),
        ],
        compiler_params=pltpu.CompilerParams(
            collective_id=0, has_side_effects=True, vmem_limit_bytes=16 * 1024 * 1024
        ),
    )(patch_slot, chunk, green_tiles[0])
    return result[None]


def solution(mesh):
    in_specs = (P("patch", "site", None), P("site", "patch", None, None), P())
    out_specs = P("site", "patch", None, None)
    return jax.shard_map(
        functools.partial(local, mesh.shape["site"], mesh.shape["patch"]),
        mesh=mesh, in_specs=in_specs, out_specs=out_specs, check_vma=False,
    )
```

```python
import functools

import jax
import jax.numpy as jnp
from jax import lax
from jax.experimental import pallas as pl
from jax.experimental.pallas import tpu as pltpu
from jax.sharding import PartitionSpec as P

MESH = pl.DeviceIdType.MESH
BLOCK = 32
LANES = 128


ARRIVAL = (1, 3, 2, 4, 6, 5, 7, 8)


def z_slot(direction, k):
    return 1 + 2 * ARRIVAL.index(k) + (direction < 0)


def z_hop(k):
    return 2 if k == 8 else (3, 1, 1)[k % 3]


def kernel(
    nz, npd, slots_hbm, slip_ref, green_hbm, out_ref,
    slots, places, green_ref, gath, outg, arrived, tiles_ref, band, prod, part, recv,
    lsem, zsend, zrecv, gsend, grecv, psend, precv, rsend, rrecv,
):
    z = lax.axis_index("site")
    me = lax.axis_index("patch")
    side = 4
    chip_x, chip_y, core = me // (2 * side), lax.rem(me // 2, side), lax.rem(me, 2)
    my_chip = me // 2
    partner = me + 1 - 2 * core
    patches = slots.shape[0] // npd
    slot_width = green_ref.shape[0]
    lags = green_ref.shape[2]
    tiles = lags // LANES
    width = lags + LANES
    out_len = out_ref.shape[2]
    rows, depth = slip_ref.shape[1:]

    load_slots = pltpu.make_async_copy(slots_hbm, slots, lsem.at[0])
    load_green = pltpu.make_async_copy(green_hbm, green_ref, lsem.at[1])
    load_slots.start()
    load_green.start()

    def distance(offset):
        dx, dy, _ = offset
        return min(dx, side - dx) + min(dy, side - dy)

    offsets = [
        (dx, dy, other)
        for dx in range(side) for dy in range(side) for other in range(2)
    ]
    offsets = sorted(offsets, key=distance, reverse=True)[:-2] + [(0, 0, 1)]

    def peer_at(offset):
        dx, dy, other = offset
        chip = lax.rem(chip_x + dx, side) * side + lax.rem(chip_y + dy, side)
        return 2 * chip + (1 - core if other else core)

    barrier = pltpu.get_barrier_semaphore()
    greetings = 0
    for step in (3, nz - 3, 2, nz - 2, 1, nz - 1):
        for receiver in (me, partner) if step in (3, nz - 3, 1, nz - 1) else (me,):
            pl.semaphore_signal(
                barrier, inc=1, device_id=(lax.rem(z + step, nz), receiver), device_id_type=MESH
            )
            greetings += 1
    for offset in offsets:
        pl.semaphore_signal(
            barrier, inc=1, device_id=(z, peer_at(offset)), device_id_type=MESH
        )

    load_slots.wait()
    load_green.wait()

    def pick(device, carry):
        first, last = jnp.int32(0), jnp.int32(0)
        values = [slots[device * patches + i] for i in range(patches)]
        hits = [value // slot_width == me for value in values]
        for i in range(patches):
            last = jnp.where(hits[i], values[i], last)
            j = patches - 1 - i
            first = jnp.where(hits[j], values[j], first)
        outg[2 * device] = green_ref[first % slot_width]
        outg[2 * device + 1] = green_ref[last % slot_width]
        return carry

    lax.fori_loop(0, npd, pick, 0)

    owners = [slots[me * patches + i] // slot_width for i in range(patches)]
    for i in range(patches):
        rank = jnp.int32(0)
        for j in range(i):
            rank = jnp.where(owners[j] == owners[i], 1, rank)
        places[i] = 2 * owners[i] + rank

    pl.semaphore_wait(barrier, npd - 1 + greetings)

    def half_of(slot, half):
        return gath.at[slot, :, half * depth : (half + 1) * depth]

    swap = pltpu.make_async_remote_copy(
        src_ref=slip_ref.at[1 - core],
        dst_ref=half_of(0, 1),
        send_sem=zsend.at[0, 1],
        recv_sem=zrecv.at[0, 1],
        device_id=(z, partner),
        device_id_type=MESH,
    )
    def zcopy(direction, k, half):
        hop = z_hop(k)
        slot = z_slot(direction, k)
        target, receiver = lax.rem(z + (hop if direction == 1 else nz - hop), nz), me
        if k > hop:
            source = half_of(z_slot(direction, k - hop), half)
        elif half:
            source, receiver = slip_ref.at[1 - core], partner
        else:
            source = slip_ref.at[core]
        return pltpu.make_async_remote_copy(
            src_ref=source,
            dst_ref=half_of(slot, half),
            send_sem=zsend.at[slot, half],
            recv_sem=zrecv.at[slot, half],
            device_id=(target, receiver),
            device_id_type=MESH,
        )

    reach = {1: nz // 2, -1: nz - 1 - nz // 2}

    def zgo(k, half):
        for direction in (1, -1):
            if k <= reach[direction]:
                zcopy(direction, k, half).start()

    def zwait(k, half):
        for direction in (1, -1):
            if k <= reach[direction]:
                zcopy(direction, k, half).wait_recv()

    def zrelay(k, after):
        for half in range(2):
            zwait(k, half)
            for onward in after:
                zgo(onward, half)

    for k in (3, 1):
        for half in range(2):
            zgo(k, half)
    swap.start()
    gath[0, :, 0:depth] = slip_ref[core]

    def gcopy(peer):
        return pltpu.make_async_remote_copy(
            src_ref=outg.at[pl.ds(2 * peer, 2)],
            dst_ref=arrived.at[pl.ds(2 * me, 2)],
            send_sem=gsend.at[peer],
            recv_sem=grecv.at[me],
            device_id=(z, peer),
            device_id_type=MESH,
        )

    for offset in offsets:
        gcopy(peer_at(offset)).start()
    keep = pltpu.make_async_copy(
        outg.at[pl.ds(2 * me, 2)], arrived.at[pl.ds(2 * me, 2)], grecv.at[me]
    )
    keep.start()

    def gwait(i, carry):
        pltpu.make_async_copy(
            outg.at[pl.ds(2 * i, 2)], arrived.at[pl.ds(2 * i, 2)], grecv.at[i]
        ).wait()
        return carry

    row_of = lax.broadcasted_iota(jnp.int32, (BLOCK, LANES), 0)
    lane_of = lax.broadcasted_iota(jnp.int32, (BLOCK, LANES), 1)
    inside = lane_of >= row_of

    def select(p, carry):
        tiles_ref[p] = arrived[places[p]]
        return carry

    share = pltpu.make_async_remote_copy(
        src_ref=tiles_ref.at[0:patches],
        dst_ref=tiles_ref.at[patches : 2 * patches],
        send_sem=psend,
        recv_sem=precv,
        device_id=(z, partner),
        device_id_type=MESH,
    )

    def build(p, carry):
        tile = tiles_ref[p].astype(jnp.float32)
        at = pl.multiple_of(p * BLOCK, BLOCK)
        for c in range(2):
            before = jnp.zeros((BLOCK, LANES), jnp.float32)
            for m in range(tiles + 1):
                if m < tiles:
                    row = tile[c : c + 1, m * LANES : (m + 1) * LANES]
                    turned = pltpu.roll(
                        jnp.broadcast_to(row, (BLOCK, LANES)), 0, 1, stride=1, stride_axis=0
                    )
                else:
                    turned = jnp.zeros((BLOCK, LANES), jnp.float32)
                block = jnp.where(inside, turned, before)
                before = turned
                start = c * width + m * LANES
                band[pl.ds(at, BLOCK), start : start + LANES] = block.astype(jnp.bfloat16)
        return carry

    zrelay(1, (2,))
    zrelay(3, (6, 4))
    lax.fori_loop(0, npd, gwait, 0)
    lax.fori_loop(0, patches, select, 0)
    share.start()
    lax.fori_loop(0, patches, build, 0)
    zrelay(4, (5,))
    zrelay(6, (8, 7))
    share.wait_recv()
    lax.fori_loop(patches, 2 * patches, build, 0)

    sub = lax.broadcasted_iota(jnp.int32, (8, out_len), 0)
    pad = jnp.zeros((8, LANES), jnp.float32)

    def rcopy(slot):
        chip = chip_of(slot)
        return chip, pltpu.make_async_remote_copy(
            src_ref=part.at[slot],
            dst_ref=recv.at[my_chip],
            send_sem=rsend.at[slot],
            recv_sem=rrecv.at[my_chip],
            device_id=(z, 2 * chip + core),
            device_id_type=MESH,
        )

    def chip_of(slot):
        if slot == 0:
            return z
        k = ARRIVAL[(slot - 1) // 2]
        return lax.rem(z + (nz - k if slot % 2 else k), nz)

    def compute(first, last):
        count = last - first
        left = gath[first:last].reshape(count * rows, 2 * depth)
        step = 256
        for n in range(0, 2 * width, step):
            prod[0 : count * rows, n : n + step] = jnp.dot(
                left, band[:, n : n + step], preferred_element_type=jnp.float32
            )
        for slot in range(first, last):
            base = (slot - first) * rows
            sums, turned = [], []
            for c in range(2):
                low, high = [
                    prod[base + 8 * i : base + 8 * i + 8, c * width : (c + 1) * width]
                    for i in range(2)
                ]
                total = jnp.concatenate([low, pad], 1) + jnp.concatenate([pad, high], 1)
                sums.append(total)
                turned.append(pltpu.roll(total, 2 * BLOCK, 1))
            both = jnp.where(sub < 4, sums[0], pltpu.roll(sums[1], 4, 0)) + jnp.where(
                sub < 4, pltpu.roll(turned[0], 4, 0), turned[1]
            )
            result = both + pltpu.roll(pltpu.roll(both, BLOCK, 1), 6, 0)
            part[slot, 0:2] = result[0:2]
            part[slot, 2:4] = result[4:6]
            chip, copy = rcopy(slot)

            @pl.when(chip != my_chip)
            def _():
                copy.start()

            @pl.when(chip == my_chip)
            def _():
                pltpu.make_async_copy(part.at[slot], recv.at[my_chip], rrecv.at[my_chip]).start()

    def both(k):
        zwait(k, 0)
        zwait(k, 1)

    swap.wait_recv()
    both(2)
    compute(0, 7)
    both(5)
    compute(7, 13)
    both(7)
    both(8)
    compute(13, 16)

    def rwait(i, carry):
        pltpu.make_async_copy(part.at[i], recv.at[i], rrecv.at[i]).wait()
        return carry

    lax.fori_loop(0, nz, rwait, 0)
    total = jnp.sum(recv[...], axis=0)
    for v in range(2):
        for c in range(2):
            out_ref[v, c : c + 1] = total[2 * c + v : 2 * c + v + 1]

    swap.wait_send()
    share.wait_send()
    for direction in (1, -1):
        for k in range(1, reach[direction] + 1):
            for half in range(2):
                zcopy(direction, k, half).wait_send()

    def gdrain(i, carry):
        @pl.when(i != me)
        def _():
            gcopy(i).wait_send()

        return carry

    lax.fori_loop(0, npd, gdrain, 0)
    for slot in range(nz):
        chip, copy = rcopy(slot)

        @pl.when(chip != my_chip)
        def _():
            copy.wait_send()


def local(nz, npd, slip_rates, green_tiles, patch_slot):
    patches, own_v, samples = slip_rates.shape
    lags = green_tiles.shape[3]
    blocks = samples // BLOCK
    assert own_v == 4 and blocks == 8 and npd == 2 * nz and nz == 16
    rows, depth = blocks * 2, patches * BLOCK
    chunk = (
        slip_rates.reshape(patches, 2, 2, blocks, BLOCK)
        .transpose(1, 3, 2, 0, 4)
        .reshape(2, rows, depth)
    )
    width, out_len = lags + LANES, lags + samples
    vmem = pl.BlockSpec(memory_space=pltpu.VMEM)
    hbm = pl.BlockSpec(memory_space=pltpu.HBM)
    dma = pltpu.SemaphoreType.DMA
    result = pl.pallas_call(
        functools.partial(kernel, nz, npd),
        out_shape=jax.ShapeDtypeStruct((2, 2, out_len), jnp.float32),
        in_specs=[hbm, vmem, hbm],
        out_specs=vmem,
        scratch_shapes=[
            pltpu.SMEM(patch_slot.shape, jnp.int32),
            pltpu.SMEM((patches,), jnp.int32),
            pltpu.VMEM(green_tiles.shape[1:], jnp.bfloat16),
            pltpu.VMEM((nz, rows, 2 * depth), jnp.bfloat16),
            pltpu.VMEM((2 * npd, 2, lags), jnp.bfloat16),
            pltpu.VMEM((2 * npd, 2, lags), jnp.bfloat16),
            pltpu.VMEM((2 * patches, 2, lags), jnp.bfloat16),
            pltpu.VMEM((2 * depth, 2 * width), jnp.bfloat16),
            pltpu.VMEM((7 * rows, 2 * width), jnp.float32),
            pltpu.VMEM((nz, 4, out_len), jnp.float32),
            pltpu.VMEM((nz, 4, out_len), jnp.float32),
            dma((2,)), dma((nz, 2)), dma((nz, 2)), dma((npd,)), dma((npd,)),
            dma, dma, dma((nz,)), dma((nz,)),
        ],
        compiler_params=pltpu.CompilerParams(
            collective_id=0, has_side_effects=True, vmem_limit_bytes=16 * 1024 * 1024
        ),
    )(pltpu.with_memory_space_constraint(patch_slot, pltpu.HBM), chunk, pltpu.with_memory_space_constraint(green_tiles[0], pltpu.HBM))
    return result[None]


def solution(mesh):
    in_specs = (P("patch", "site", None), P("site", "patch", None, None), P())
    out_specs = P("site", "patch", None, None)
    return jax.shard_map(
        functools.partial(local, mesh.shape["site"], mesh.shape["patch"]),
        mesh=mesh, in_specs=in_specs, out_specs=out_specs, check_vma=False,
    )
```

```python
import functools

import jax
import jax.numpy as jnp
from jax import lax
from jax.experimental import pallas as pl
from jax.experimental.pallas import tpu as pltpu
from jax.sharding import PartitionSpec as P

MESH = pl.DeviceIdType.MESH
BLOCK = 32
LANES = 128


ARRIVAL = (1, 3, 2, 4, 6, 5, 7, 8)


def z_slot(direction, k):
    return 1 + 2 * ARRIVAL.index(k) + (direction < 0)


def z_hop(k):
    return 2 if k == 8 else (3, 1, 1)[k % 3]


def kernel(
    nz, npd, slots_hbm, slip_ref, green_hbm, out_ref,
    slots, places, green_ref, gath, outg, arrived, tiles_ref, band, prod, part, recv,
    lsem, zsend, zrecv, gsend, grecv, psend, precv, rsend, rrecv,
):
    z = lax.axis_index("site")
    me = lax.axis_index("patch")
    side = 4
    chip_x, chip_y, core = me // (2 * side), lax.rem(me // 2, side), lax.rem(me, 2)
    my_chip = me // 2
    partner = me + 1 - 2 * core
    patches = slots.shape[0] // npd
    slot_width = green_ref.shape[0]
    lags = green_ref.shape[2]
    tiles = lags // LANES
    width = lags + LANES
    out_len = out_ref.shape[2]
    rows, depth = slip_ref.shape[1:]

    load_slots = pltpu.make_async_copy(slots_hbm, slots, lsem.at[0])
    load_green = pltpu.make_async_copy(green_hbm, green_ref, lsem.at[1])
    load_slots.start()
    load_green.start()

    def distance(offset):
        dx, dy, _ = offset
        return min(dx, side - dx) + min(dy, side - dy)

    offsets = [
        (dx, dy, other)
        for dx in range(side) for dy in range(side) for other in range(2)
    ]
    offsets = sorted(offsets, key=distance, reverse=True)[:-2] + [(0, 0, 1)]

    def peer_at(offset):
        dx, dy, other = offset
        chip = lax.rem(chip_x + dx, side) * side + lax.rem(chip_y + dy, side)
        return 2 * chip + (1 - core if other else core)

    barrier = pltpu.get_barrier_semaphore()
    greetings = 0
    for step in (3, nz - 3, 2, nz - 2, 1, nz - 1):
        for receiver in (me, partner) if step in (3, nz - 3, 1, nz - 1) else (me,):
            pl.semaphore_signal(
                barrier, inc=1, device_id=(lax.rem(z + step, nz), receiver), device_id_type=MESH
            )
            greetings += 1
    for offset in offsets:
        pl.semaphore_signal(
            barrier, inc=1, device_id=(z, peer_at(offset)), device_id_type=MESH
        )

    load_slots.wait()
    load_green.wait()

    def pick(device, carry):
        first, last = jnp.int32(0), jnp.int32(0)
        values = [slots[device * patches + i] for i in range(patches)]
        hits = [value // slot_width == me for value in values]
        for i in range(patches):
            last = jnp.where(hits[i], values[i], last)
            j = patches - 1 - i
            first = jnp.where(hits[j], values[j], first)
        outg[2 * device] = green_ref[first % slot_width]
        outg[2 * device + 1] = green_ref[last % slot_width]
        return carry

    lax.fori_loop(0, npd, pick, 0)

    owners = [slots[me * patches + i] // slot_width for i in range(patches)]
    for i in range(patches):
        rank = jnp.int32(0)
        for j in range(i):
            rank = jnp.where(owners[j] == owners[i], 1, rank)
        places[i] = 2 * owners[i] + rank

    pl.semaphore_wait(barrier, npd - 1 + greetings)

    def half_of(slot, half):
        return gath.at[slot, :, half * depth : (half + 1) * depth]

    swap = pltpu.make_async_remote_copy(
        src_ref=slip_ref.at[1 - core],
        dst_ref=half_of(0, 1),
        send_sem=zsend.at[0, 1],
        recv_sem=zrecv.at[0, 1],
        device_id=(z, partner),
        device_id_type=MESH,
    )
    def zcopy(direction, k, half):
        hop = z_hop(k)
        slot = z_slot(direction, k)
        target, receiver = lax.rem(z + (hop if direction == 1 else nz - hop), nz), me
        if k > hop:
            source = half_of(z_slot(direction, k - hop), half)
        elif half:
            source, receiver = slip_ref.at[1 - core], partner
        else:
            source = slip_ref.at[core]
        return pltpu.make_async_remote_copy(
            src_ref=source,
            dst_ref=half_of(slot, half),
            send_sem=zsend.at[slot, half],
            recv_sem=zrecv.at[slot, half],
            device_id=(target, receiver),
            device_id_type=MESH,
        )

    reach = {1: nz // 2, -1: nz - 1 - nz // 2}

    def zgo(k, half):
        for direction in (1, -1):
            if k <= reach[direction]:
                zcopy(direction, k, half).start()

    def zwait(k, half):
        for direction in (1, -1):
            if k <= reach[direction]:
                zcopy(direction, k, half).wait_recv()

    def zrelay(k, after):
        for half in range(2):
            zwait(k, half)
            for onward in after:
                zgo(onward, half)

    for k in (3, 1):
        for half in range(2):
            zgo(k, half)
    swap.start()
    gath[0, :, 0:depth] = slip_ref[core]

    def gcopy(peer):
        return pltpu.make_async_remote_copy(
            src_ref=outg.at[pl.ds(2 * peer, 2)],
            dst_ref=arrived.at[pl.ds(2 * me, 2)],
            send_sem=gsend.at[peer],
            recv_sem=grecv.at[me],
            device_id=(z, peer),
            device_id_type=MESH,
        )

    for offset in offsets:
        gcopy(peer_at(offset)).start()
    keep = pltpu.make_async_copy(
        outg.at[pl.ds(2 * me, 2)], arrived.at[pl.ds(2 * me, 2)], grecv.at[me]
    )
    keep.start()

    def gwait(i, carry):
        pltpu.make_async_copy(
            outg.at[pl.ds(2 * i, 2)], arrived.at[pl.ds(2 * i, 2)], grecv.at[i]
        ).wait()
        return carry

    row_of = lax.broadcasted_iota(jnp.int32, (BLOCK, LANES), 0)
    lane_of = lax.broadcasted_iota(jnp.int32, (BLOCK, LANES), 1)
    inside = lane_of >= row_of

    def select(p, carry):
        tiles_ref[p] = arrived[places[p]]
        return carry

    share = pltpu.make_async_remote_copy(
        src_ref=tiles_ref.at[0:patches],
        dst_ref=tiles_ref.at[patches : 2 * patches],
        send_sem=psend,
        recv_sem=precv,
        device_id=(z, partner),
        device_id_type=MESH,
    )

    def build(p, carry):
        tile = tiles_ref[p].astype(jnp.float32)
        at = pl.multiple_of(p * BLOCK, BLOCK)
        for c in range(2):
            before = jnp.zeros((BLOCK, LANES), jnp.float32)
            for m in range(tiles + 1):
                if m < tiles:
                    row = tile[c : c + 1, m * LANES : (m + 1) * LANES]
                    turned = pltpu.roll(
                        jnp.broadcast_to(row, (BLOCK, LANES)), 0, 1, stride=1, stride_axis=0
                    )
                else:
                    turned = jnp.zeros((BLOCK, LANES), jnp.float32)
                block = jnp.where(inside, turned, before)
                before = turned
                start = c * width + m * LANES
                band[pl.ds(at, BLOCK), start : start + LANES] = block.astype(jnp.bfloat16)
        return carry

    zrelay(1, (2,))
    zrelay(3, (6, 4))
    lax.fori_loop(0, npd, gwait, 0)
    lax.fori_loop(0, patches, select, 0)
    share.start()
    lax.fori_loop(0, patches, build, 0, unroll=4)
    zrelay(4, (5,))
    zrelay(6, (8, 7))
    share.wait_recv()
    lax.fori_loop(patches, 2 * patches, build, 0, unroll=4)

    sub = lax.broadcasted_iota(jnp.int32, (8, out_len), 0)
    pad = jnp.zeros((8, LANES), jnp.float32)

    def rcopy(slot):
        chip = chip_of(slot)
        return chip, pltpu.make_async_remote_copy(
            src_ref=part.at[slot],
            dst_ref=recv.at[my_chip],
            send_sem=rsend.at[slot],
            recv_sem=rrecv.at[my_chip],
            device_id=(z, 2 * chip + core),
            device_id_type=MESH,
        )

    def chip_of(slot):
        if slot == 0:
            return z
        k = ARRIVAL[(slot - 1) // 2]
        return lax.rem(z + (nz - k if slot % 2 else k), nz)

    def compute(first, last):
        count = last - first
        left = gath[first:last].reshape(count * rows, 2 * depth)
        step = 256
        for n in range(0, 2 * width, step):
            prod[0 : count * rows, n : n + step] = jnp.dot(
                left, band[:, n : n + step], preferred_element_type=jnp.float32
            )
        for slot in range(first, last):
            base = (slot - first) * rows
            sums, turned = [], []
            for c in range(2):
                low, high = [
                    prod[base + 8 * i : base + 8 * i + 8, c * width : (c + 1) * width]
                    for i in range(2)
                ]
                total = jnp.concatenate([low, pad], 1) + jnp.concatenate([pad, high], 1)
                sums.append(total)
                turned.append(pltpu.roll(total, 2 * BLOCK, 1))
            both = jnp.where(sub < 4, sums[0], pltpu.roll(sums[1], 4, 0)) + jnp.where(
                sub < 4, pltpu.roll(turned[0], 4, 0), turned[1]
            )
            result = both + pltpu.roll(pltpu.roll(both, BLOCK, 1), 6, 0)
            part[slot, 0:2] = result[0:2]
            part[slot, 2:4] = result[4:6]
            chip, copy = rcopy(slot)

            @pl.when(chip != my_chip)
            def _():
                copy.start()

            @pl.when(chip == my_chip)
            def _():
                pltpu.make_async_copy(part.at[slot], recv.at[my_chip], rrecv.at[my_chip]).start()

    def both(k):
        zwait(k, 0)
        zwait(k, 1)

    swap.wait_recv()
    both(2)
    compute(0, 7)
    both(5)
    compute(7, 13)
    both(7)
    both(8)
    compute(13, 16)

    def rwait(i, carry):
        pltpu.make_async_copy(part.at[i], recv.at[i], rrecv.at[i]).wait()
        return carry

    lax.fori_loop(0, nz, rwait, 0)
    total = jnp.sum(recv[...], axis=0)
    for v in range(2):
        for c in range(2):
            out_ref[v, c : c + 1] = total[2 * c + v : 2 * c + v + 1]

    swap.wait_send()
    share.wait_send()
    for direction in (1, -1):
        for k in range(1, reach[direction] + 1):
            for half in range(2):
                zcopy(direction, k, half).wait_send()

    def gdrain(i, carry):
        @pl.when(i != me)
        def _():
            gcopy(i).wait_send()

        return carry

    lax.fori_loop(0, npd, gdrain, 0)
    for slot in range(nz):
        chip, copy = rcopy(slot)

        @pl.when(chip != my_chip)
        def _():
            copy.wait_send()


def local(nz, npd, slip_rates, green_tiles, patch_slot):
    patches, own_v, samples = slip_rates.shape
    lags = green_tiles.shape[3]
    blocks = samples // BLOCK
    assert own_v == 4 and blocks == 8 and npd == 2 * nz and nz == 16
    rows, depth = blocks * 2, patches * BLOCK
    chunk = (
        slip_rates.reshape(patches, 2, 2, blocks, BLOCK)
        .transpose(1, 3, 2, 0, 4)
        .reshape(2, rows, depth)
    )
    width, out_len = lags + LANES, lags + samples
    vmem = pl.BlockSpec(memory_space=pltpu.VMEM)
    hbm = pl.BlockSpec(memory_space=pltpu.HBM)
    dma = pltpu.SemaphoreType.DMA
    result = pl.pallas_call(
        functools.partial(kernel, nz, npd),
        out_shape=jax.ShapeDtypeStruct((2, 2, out_len), jnp.float32),
        in_specs=[hbm, vmem, hbm],
        out_specs=vmem,
        scratch_shapes=[
            pltpu.SMEM(patch_slot.shape, jnp.int32),
            pltpu.SMEM((patches,), jnp.int32),
            pltpu.VMEM(green_tiles.shape[1:], jnp.bfloat16),
            pltpu.VMEM((nz, rows, 2 * depth), jnp.bfloat16),
            pltpu.VMEM((2 * npd, 2, lags), jnp.bfloat16),
            pltpu.VMEM((2 * npd, 2, lags), jnp.bfloat16),
            pltpu.VMEM((2 * patches, 2, lags), jnp.bfloat16),
            pltpu.VMEM((2 * depth, 2 * width), jnp.bfloat16),
            pltpu.VMEM((7 * rows, 2 * width), jnp.float32),
            pltpu.VMEM((nz, 4, out_len), jnp.float32),
            pltpu.VMEM((nz, 4, out_len), jnp.float32),
            dma((2,)), dma((nz, 2)), dma((nz, 2)), dma((npd,)), dma((npd,)),
            dma, dma, dma((nz,)), dma((nz,)),
        ],
        compiler_params=pltpu.CompilerParams(
            collective_id=0, has_side_effects=True, vmem_limit_bytes=16 * 1024 * 1024
        ),
    )(pltpu.with_memory_space_constraint(patch_slot, pltpu.HBM), chunk, pltpu.with_memory_space_constraint(green_tiles[0], pltpu.HBM))
    return result[None]


def solution(mesh):
    in_specs = (P("patch", "site", None), P("site", "patch", None, None), P())
    out_specs = P("site", "patch", None, None)
    return jax.shard_map(
        functools.partial(local, mesh.shape["site"], mesh.shape["patch"]),
        mesh=mesh, in_specs=in_specs, out_specs=out_specs, check_vma=False,
    )
```
